512 devices in a mesh: chan: 64 (over z, y_lo, x), facet: 8 (over y_hi, core).
Axes of the slice: x: 4, y: 8 (y_hi: 4, y_lo: 2; y = y_hi * 2 + y_lo), z: 8, core: 2. Of those that a mesh axis runs over, the one named last changes fastest.
Arguments:
- estimate: float32 [256, 128, 1024], P('chan', None, 'facet'), may hold values from -16 to 16
- dirty: float32 [256, 128, 1024], P('chan', None, 'facet'), may hold values from -16 to 16
- weights: float32 [256, 128, 1024], P('chan', None, 'facet'), may hold values from 0.2 to 1
- margin: int32 [8], replicated, may hold values from 1 to 16, as said below
- blend_table: int32 [8, 160], replicated, may hold values from 1 to 8
- tau_steps: int32 [2], replicated, may hold values from 1 to 4
Outputs:
- updated: float32 [256, 128, 1024], P('chan', None, 'facet')
The draws below stay inside these ranges and needn't reach their ends.
Inputs may be any that keep to these rules, and one draw needn't show every extreme that they name: Some facet has margin exactly 16.
All inputs are finite; a program needn't handle non-finite values.
Results may differ from the reference program's by a relative error of at most 0.00012.
Values sent between devices are 32-bit elements; how exact they have to be, the bound alone decides.
No kernel may reach another device: no remote copies, remote signals or barrier semaphores. Data moves between devices by JAX's collectives and lax.ppermute only.
A program may use at most 64 MiB of HBM per device.

```python
import math
import jax
import jax.numpy as jnp
from jax import lax

C = 256
W = 128
HD = 128
OV = 16
NS_STEPS = 2
ITERS = 2
FACETS = 8
H = 1024


def draw_margin(key, part):
    first_key = jax.random.fold_in(key, 11)
    second_key = jax.random.fold_in(key, 23)
    widths = jax.random.randint(first_key, (FACETS,), 1, OV + 1)
    chosen = jax.random.randint(second_key, (), 0, FACETS)
    return jnp.where(jnp.arange(FACETS) == chosen, OV, widths).astype(jnp.int32)


def plant(result, own_key, low, largest):
    index_at = [jax.random.randint(jax.random.fold_in(own_key, axis), (), 0, length) for axis, length in enumerate(result.shape)]
    longest = result.shape.index(max(result.shape))
    next_to = index_at[:longest] + [(index_at[longest] + 1) % result.shape[longest]] + index_at[longest + 1:]
    return result.at[tuple(index_at)].set(low).at[tuple(next_to)].set(largest)


def raised(values, rng, source, target, shards_of, factor):
    owner, partner = [(jnp.arange(values.shape[dim]) // (values.shape[dim] // shards_of)).reshape([-1 if axis == dim else 1 for axis in range(values.ndim)]) for dim in (source, target)]
    chosen = jax.random.permutation(rng, shards_of)[partner]
    strong = (owner == chosen) | (owner == (partner + shards_of // 2) % shards_of)
    return jnp.where(strong, factor * values, values)


def level_of(key, shape, shards, smallest, high):
    def one(dim, blocks):
        steps = jax.random.uniform(jax.random.fold_in(jax.random.fold_in(key, 6), dim), (blocks,), jnp.float32, smallest / len(shards), high / len(shards))
        return jnp.repeat(jnp.exp(steps), shape[dim] // blocks).reshape((-1,) + (1,) * (len(shape) - dim - 1))

    loudness = one(*shards[0])
    for cut in shards[1:]:
        loudness = loudness * one(*cut)
    return loudness


def heavy_noise(rng, shape, spread, most, pieces, heavy, kind=jnp.bfloat16):
    entries = spread * jax.random.normal(rng, shape, jnp.float32)
    if pieces:
        entries = entries * level_of(rng, shape, pieces, -0.22, 0.18)
    return jnp.clip(raised(entries, jax.random.fold_in(rng, 3), *heavy), -most, most).astype(kind)


def setup_inputs(seed: int = 0) -> dict:
    splits = jax.random.split(jax.random.key(seed), 7)
    estimate = heavy_noise(splits[0], (C, W, H), 1.0, 16.0, ((0, 64), (2, 8)), (1, 0, 64, 4.0), jnp.float32)
    dirty = heavy_noise(splits[1], (C, W, H), 1.0, 16.0, ((0, 64), (2, 8)), (2, 0, 64, 4.0), jnp.float32)
    weights = jnp.clip(jnp.exp(math.log(1.0) - 1.609438 * jax.random.uniform(splits[2], (C, W, H), jnp.float32) ** level_of(splits[2], (C, W, H), ((0, 64), (2, 8)), -0.2, 0.2)), 0.2, 1.0)
    margin = draw_margin(jax.random.fold_in(splits[6], 71), 0)
    blend_table = plant(jax.random.randint(splits[4], (FACETS, HD + 2 * OV), 1, 9), jax.random.fold_in(splits[4], 1), 1, 8).astype(jnp.int32)
    tau_steps = jax.random.randint(splits[5], (ITERS,), 1, 5).astype(jnp.int32)
    return {"estimate": estimate, "dirty": dirty, "weights": weights, "margin": margin, "blend_table": blend_table, "tau_steps": tau_steps}


def apply_shrink(gram, columns, tau_value):
    channel_count = gram.shape[0]
    identity = jnp.eye(channel_count, dtype=jnp.float32)
    mean_eigen = jnp.trace(gram) / channel_count + 1e-06
    target = (gram + 0.01 * mean_eigen * identity) / (16.16 * mean_eigen)
    inverse_root = identity
    for newton_step in range(NS_STEPS):
        middle = 1.5 * identity - 0.5 * jnp.dot(inverse_root, target, precision=lax.Precision.HIGHEST)
        target = jnp.dot(target, middle, precision=lax.Precision.HIGHEST)
        inverse_root = jnp.dot(middle, inverse_root, precision=lax.Precision.HIGHEST)
    factor = 0.1 * tau_value / math.sqrt(1.01)
    kernel = identity - factor * inverse_root
    return jnp.dot(kernel, columns, precision=lax.Precision.HIGHEST)

def reference(estimate, dirty, weights, margin, blend_table, tau_steps):
    channel_count, image_width, height = estimate.shape
    center = HD
    ext_len = center + 2 * OV
    row_index = jnp.arange(ext_len, dtype=jnp.int32)
    current = estimate
    for iteration in range(ITERS):
        tau_value = tau_steps[iteration].astype(jnp.float32)
        moved_cube = current - weights * (current - dirty)
        padded = jnp.pad(moved_cube, ((0, 0), (0, 0), (OV, OV)))
        numerator = jnp.zeros_like(padded)
        denominator = jnp.zeros((height + 2 * OV,), jnp.float32)
        for facet_index in range(FACETS):
            width_here = margin[facet_index]
            row_mask = ((row_index >= OV - width_here) & (row_index < center + OV + width_here)).astype(jnp.float32)
            first_row = facet_index * center
            block = padded[:, :, first_row:first_row + ext_len] * row_mask
            columns = block.reshape(channel_count, -1)
            gram = jnp.dot(columns, columns.T, precision=lax.Precision.HIGHEST)
            shrunk = apply_shrink(gram, columns, tau_value).reshape(block.shape)
            row_weight = blend_table[facet_index].astype(jnp.float32) * row_mask
            numerator = numerator.at[:, :, first_row:first_row + ext_len].add(shrunk * row_weight)
            denominator = denominator.at[first_row:first_row + ext_len].add(row_weight)
        current = numerator[:, :, OV:OV + height] / denominator[OV:OV + height]
    return current
```

```python
import math

import jax
import jax.numpy as jnp
from jax import lax
from jax.sharding import PartitionSpec as P

OV = 16
NS_STEPS = 2
ITERS = 2
HI = lax.Precision.HIGHEST


def to_pixels(stack, n):
    a, cl, w, hd = stack.shape
    wl = w // n
    sent = stack.reshape(a, cl, n, wl, hd).transpose(2, 0, 1, 3, 4).reshape(n, a * cl * wl, hd)
    got = lax.all_to_all(sent, "chan", 0, 0)
    return got.reshape(n, a, cl, wl, hd).transpose(1, 0, 2, 3, 4).reshape(a, n * cl, wl, hd)


def to_channels(pix, n):
    c, wl, hd = pix.shape
    cl = c // n
    got = lax.all_to_all(pix.reshape(n, cl * wl, hd), "chan", 0, 0)
    return got.reshape(n, cl, wl, hd).transpose(1, 0, 2, 3).reshape(cl, n * wl, hd)


def swap(low, high):
    size = lax.axis_size("facet")
    up = [(i, i + 1) for i in range(size - 1)]
    down = [(i + 1, i) for i in range(size - 1)]
    shape = low.shape

    def move(x, pairs):
        return lax.ppermute(x.reshape(-1, 128), "facet", pairs).reshape(shape)

    return move(high, up), move(low, down)


def total_gram(partial, n):
    c = partial.shape[0]
    tiles = partial.reshape(c // 8, 8, c // 128, 128).transpose(0, 2, 1, 3).reshape(n, -1, 128)
    mine = jnp.sum(lax.all_to_all(tiles, "chan", 0, 0), axis=0)
    every = lax.all_to_all(jnp.broadcast_to(mine[None], tiles.shape), "chan", 0, 0)
    return every.reshape(c // 8, c // 128, 8, 128).transpose(0, 2, 1, 3).reshape(c, c)


def shrink_kernel(gram, tau_value):
    channel_count = gram.shape[0]
    identity = jnp.eye(channel_count, dtype=jnp.float32)
    mean_eigen = jnp.trace(gram) / channel_count + 1e-06
    target = (gram + 0.01 * mean_eigen * identity) / (16.16 * mean_eigen)
    inverse_root = identity
    for newton_step in range(NS_STEPS):
        middle = 1.5 * identity - 0.5 * jnp.dot(inverse_root, target, precision=HI)
        if newton_step + 1 < NS_STEPS:
            target = jnp.dot(target, middle, precision=HI)
        inverse_root = jnp.dot(middle, inverse_root, precision=HI)
    factor = 0.1 * tau_value / math.sqrt(1.01)
    return identity - factor * inverse_root


def per_device(estimate, dirty, weights, margin, blend_table, tau_steps):
    n = lax.axis_size("chan")
    facet_id = lax.axis_index("facet")
    facet_total = lax.axis_size("facet")
    center = estimate.shape[2]
    ext_len = center + 2 * OV
    row_index = jnp.arange(ext_len, dtype=jnp.int32)[None, :]
    keep_all = (
        (row_index >= OV - margin[:, None]) & (row_index < center + OV + margin[:, None])
    ).astype(jnp.float32)
    weight_all = blend_table.astype(jnp.float32) * keep_all
    keep_rows = keep_all[facet_id]
    row_weight = weight_all[facet_id]
    before = weight_all[jnp.maximum(facet_id - 1, 0)][center:] * (facet_id > 0)
    after = weight_all[jnp.minimum(facet_id + 1, facet_total - 1)][: 2 * OV] * (
        facet_id < facet_total - 1
    )
    denominator = row_weight + jnp.concatenate(
        [before, jnp.zeros((center - 2 * OV,), jnp.float32), after]
    )
    denominator = jnp.where(denominator == 0.0, 1.0, denominator)

    moved = estimate - weights * (estimate - dirty)
    stack = to_pixels(jnp.stack([moved, dirty, weights]), n)
    from_before, from_after = swap(stack[..., :OV], stack[..., center - OV :])
    stack = jnp.concatenate([from_before, stack, from_after], axis=-1)
    moved, dirty, weights = stack[0], stack[1], stack[2]
    for iteration in range(ITERS):
        tau_value = tau_steps[iteration].astype(jnp.float32)
        block = moved * keep_rows
        columns = block.reshape(block.shape[0], -1)
        gram = total_gram(jnp.dot(columns, columns.T, precision=HI), n)
        shrunk = jnp.dot(shrink_kernel(gram, tau_value), columns, precision=HI).reshape(block.shape)
        weighted = shrunk * row_weight
        last = iteration + 1 == ITERS
        if last:
            from_before, from_after = swap(weighted[..., :OV], weighted[..., center + OV :])
            middle = weighted[..., OV : OV + center]
            gap = jnp.zeros(middle.shape[:-1] + (center - 2 * OV,), jnp.float32)
            middle = middle + jnp.concatenate([from_before, gap, from_after], axis=-1)
            current = middle / denominator[OV : OV + center]
        else:
            from_before, from_after = swap(weighted[..., : 2 * OV], weighted[..., center:])
            gap = jnp.zeros(weighted.shape[:-1] + (center - 2 * OV,), jnp.float32)
            current = weighted + jnp.concatenate([from_before, gap, from_after], axis=-1)
            current = current / denominator
            moved = current - weights * (current - dirty)
    return to_channels(current, n)


def solution(mesh):
    placed = (
        P("chan", None, "facet"),
        P("chan", None, "facet"),
        P("chan", None, "facet"),
        P(),
        P(),
        P(),
    )
    return jax.shard_map(
        per_device, mesh=mesh, in_specs=placed, out_specs=P("chan", None, "facet"), check_vma=False
    )
```

```python
import math

import jax
import jax.numpy as jnp
from jax import lax
from jax.experimental import pallas as pl
from jax.experimental.pallas import tpu as pltpu
from jax.sharding import PartitionSpec as P


OV = 16
CL = 4
WL = 2
HD = 128
G8 = CL * WL
ARRAYS = 3
HI = lax.Precision.HIGHEST
F32 = jnp.float32


def lanes(shape):
    return lax.broadcasted_iota(jnp.int32, shape, 1)


def shift(x, by):
    by %= x.shape[1]
    return pltpu.roll(x, by, 1) if by else x


def pack_center(pieces, offset):
    group = lanes(pieces[0].shape) // OV
    out = shift(pieces[0], -offset)
    for g in range(1, G8):
        out = jnp.where(group == g, shift(pieces[g], OV * g - offset), out)
    return out


def pack_edges(edges, offset):
    group = lanes(edges[0].shape) // (WL * OV)
    out = shift(edges[0], -offset)
    for c in range(1, CL):
        out = jnp.where(group == c, shift(edges[c], WL * OV * c - offset), out)
    return out


def open_edges(before, after, c):
    lane = lanes(before.shape)
    step = WL * OV
    rest = jnp.where(lane < 2 * step, shift(after, step - step * c), 0.0)
    return jnp.where(lane < step, shift(before, -step * c), rest)


def open_center(before, after, g):
    lane = lanes(before.shape)
    rest = jnp.where(lane >= HD - OV, shift(after, HD - OV - OV * g), 0.0)
    return jnp.where(lane < OV, shift(before, -OV * g), rest)


def gram_of(x):
    return lax.dot_general(x, x, (((1,), (1,)), ((), ())), precision=HI, preferred_element_type=F32)


def pack_body(est, dirty, weights, out):
    n = out.shape[0] // (ARRAYS * G8)
    for c in range(CL):
        for w in range(WL):
            rows = pl.ds(c * WL * n + w, n, stride=WL)
            e, d, k = est[rows, :], dirty[rows, :], weights[rows, :]
            for a, value in enumerate((e - k * (e - d), d, k)):
                out[pl.ds(a * G8 + c * WL + w, n, stride=ARRAYS * G8), :] = value


def piece(got, a, g):
    n = got.shape[0] // (ARRAYS * G8)
    return got[pl.ds(a * G8 + g, n, stride=ARRAYS * G8), :]


def edge_body(got, low, high):
    n = low.shape[0] // ARRAYS
    for a in range(ARRAYS):
        pieces = [piece(got, a, g) for g in range(G8)]
        low[pl.ds(a * n, n), :] = pack_center(pieces, 0)
        high[pl.ds(a * n, n), :] = pack_center(pieces, HD - OV)


def gram_body(got, before, after, table, x, gram):
    n = before.shape[0] // ARRAYS
    keep = table[0:1, WL * HD :]
    for c in range(CL):
        rows = pl.ds(c * n, n)
        for w in range(WL):
            x[rows, pl.ds(w * HD, HD)] = piece(got, 0, c * WL + w)
        x[rows, pl.ds(WL * HD, HD)] = open_edges(before[pl.ds(0, n), :], after[pl.ds(0, n), :], c) * keep
    gram[...] = gram_of(x[...])


def shrink_of(gram, x, factor):
    count = gram.shape[0]
    row = lax.broadcasted_iota(jnp.int32, gram.shape, 0)
    identity = (row == lanes(gram.shape)).astype(F32)
    trace = jnp.sum(jnp.sum(gram * identity, axis=1, keepdims=True), axis=0, keepdims=True)
    mean_eigen = trace / count + 1e-06
    target = (gram + (0.01 * mean_eigen) * identity) / (16.16 * mean_eigen)
    first = 1.5 * identity - 0.5 * target
    target = jnp.dot(target, first, precision=HI)
    second = 1.5 * identity - 0.5 * jnp.dot(first, target, precision=HI)
    inverse_root = jnp.dot(second, first, precision=HI)
    return jnp.dot(identity - factor * inverse_root, x, precision=HI)


def apply_body(step, last, gram, x, table, out, low, high):
    n = x.shape[0] // CL
    factor = table[3 + step : 4 + step, : gram.shape[0]]
    out[...] = shrink_of(gram[...], x[...], factor) * table[1:2, :]
    edges = [out[pl.ds(c * n, n), pl.ds(WL * HD, HD)] for c in range(CL)]
    inner = slice(0, n) if last else slice(n, 2 * n)
    low[inner, :] = pack_edges(edges, 0)
    high[inner, :] = pack_edges(edges, WL * OV)
    if not last:
        pieces = [out[pl.ds(c * n, n), pl.ds(w * HD, HD)] for c in range(CL) for w in range(WL)]
        low[0:n, :] = pack_center(pieces, 0)
        high[0:n, :] = pack_center(pieces, HD - OV)


def next_body(got, before, after, s, s_before, s_after, table, x, gram):
    n = before.shape[0] // ARRAYS
    keep = table[0:1, WL * HD :]
    scale = table[2:3, :]
    for c in range(CL):
        rows = pl.ds(c * n, n)

        def moved(total, cols, d, k):
            current = total * scale[:, cols]
            return current - k * (current - d)

        for w in range(WL):
            g = c * WL + w
            cols = slice(w * HD, w * HD + HD)
            total = s[rows, cols] + open_center(s_before[n : 2 * n, :], s_after[n : 2 * n, :], g)
            x[rows, cols] = moved(total, cols, piece(got, 1, g), piece(got, 2, g))
        cols = slice(WL * HD, WL * HD + HD)
        total = s[rows, cols] + open_edges(s_before[0:n, :], s_after[0:n, :], c)
        d = open_edges(before[n : 2 * n, :], after[n : 2 * n, :], c)
        k = open_edges(before[2 * n :, :], after[2 * n :, :], c)
        x[rows, cols] = moved(total, cols, d, k) * keep
    gram[...] = gram_of(x[...])


def close_body(s, s_before, s_after, table, out):
    n = s_before.shape[0]
    for c in range(CL):
        for w in range(WL):
            g = c * WL + w
            total = s[pl.ds(c * n, n), pl.ds(w * HD, HD)] + open_center(s_before[...], s_after[...], g)
            out[pl.ds(g, n, stride=G8), :] = total * table[2:3, w * HD : w * HD + HD]


def unpack_body(got, out):
    n = got.shape[0] // G8
    for c in range(CL):
        for w in range(WL):
            out[pl.ds(c * WL * n + w, n, stride=WL), :] = got[pl.ds(c * WL + w, n, stride=G8), :]


def run(body, name, shapes, *args, enter=True, leave=True):
    spec = pl.BlockSpec(memory_space=pltpu.VMEM)
    outs = [pltpu.VMEM(s, F32) if leave else jax.ShapeDtypeStruct(s, F32) for s in shapes]
    single = len(outs) == 1
    if enter:
        args = [pltpu.with_memory_space_constraint(a, pltpu.VMEM) for a in args]
    return pl.pallas_call(
        body,
        out_shape=outs[0] if single else outs,
        in_specs=[spec] * len(args),
        out_specs=spec if single else [spec] * len(outs),
        name=name,
    )(*args)


def exchange(x, n):
    return lax.all_to_all(x.reshape(n, -1, HD), "chan", 0, 0).reshape(x.shape)


def swap(low, high):
    size = lax.axis_size("facet")
    up = [(i, i + 1) for i in range(size - 1)]
    down = [(i + 1, i) for i in range(size - 1)]
    return lax.ppermute(high, "facet", up), lax.ppermute(low, "facet", down)


def total_gram(partial, n):
    c = partial.shape[0]
    tiles = partial.reshape(c // 8, 8, c // 128, 128).transpose(0, 2, 1, 3).reshape(n, -1, 128)
    mine = jnp.sum(lax.all_to_all(tiles, "chan", 0, 0), axis=0)
    every = lax.all_to_all(jnp.broadcast_to(mine[None], tiles.shape), "chan", 0, 0)
    return every.reshape(c // 8, c // 128, 8, 128).transpose(0, 2, 1, 3).reshape(c, c)


def tables(margin, blend_table, tau_steps, channels):
    facet_id = lax.axis_index("facet")
    facet_total = lax.axis_size("facet")
    row_index = jnp.arange(HD + 2 * OV, dtype=jnp.int32)[None, :]
    keep_all = (
        (row_index >= OV - margin[:, None]) & (row_index < HD + OV + margin[:, None])
    ).astype(F32)
    weight_all = blend_table.astype(F32) * keep_all
    row_weight = weight_all[facet_id]
    before = weight_all[jnp.maximum(facet_id - 1, 0)][HD:] * (facet_id > 0)
    after = weight_all[jnp.minimum(facet_id + 1, facet_total - 1)][: 2 * OV] * (
        facet_id < facet_total - 1
    )
    total = row_weight + jnp.concatenate([before, jnp.zeros((HD - 2 * OV,), F32), after])
    scale = 1.0 / jnp.where(total == 0.0, 1.0, total)
    rows = jnp.stack([keep_all[facet_id], row_weight, scale])
    center, low, high = rows[:, OV : OV + HD], rows[:, :OV], rows[:, OV + HD :]
    pad = jnp.zeros((3, HD - 4 * OV), F32)
    rows = jnp.concatenate([center, center, low, low, high, high, pad], axis=1)
    factors = 0.1 * tau_steps.astype(F32) / math.sqrt(1.01)
    factors = jnp.broadcast_to(factors[:, None], (tau_steps.shape[0], rows.shape[1]))
    return jnp.concatenate([rows, factors, jnp.zeros((3, rows.shape[1]), F32)])


def per_device(estimate, dirty, weights, margin, blend_table, tau_steps):
    n = lax.axis_size("chan")
    c, width = n * CL, (WL + 1) * HD
    assert estimate.shape == (CL, n * WL, HD)
    table = tables(margin, blend_table, tau_steps, c)
    flat = (CL * WL * n, HD)
    sent = run(
        pack_body, "pack", [(ARRAYS * G8 * n, HD)], estimate.reshape(flat), dirty.reshape(flat), weights.reshape(flat), enter=False
    )
    got = exchange(sent, n)
    low, high = run(edge_body, "edges", [(ARRAYS * n, HD)] * 2, got)
    before, after = swap(low, high)
    x, gram = run(gram_body, "gram", [(c, width), (c, c)], got, before, after, table)
    gram = total_gram(gram, n)
    s, low, high = run(
        lambda *refs: apply_body(0, False, *refs), "shrink", [(c, width), (2 * n, HD), (2 * n, HD)], gram, x, table
    )
    s_before, s_after = swap(low, high)
    x, gram = run(
        next_body, "step", [(c, width), (c, c)], got, before, after, s, s_before, s_after, table
    )
    gram = total_gram(gram, n)
    s, low, high = run(
        lambda *refs: apply_body(1, True, *refs), "last", [(c, width), (n, HD), (n, HD)], gram, x, table
    )
    s_before, s_after = swap(low, high)
    back = exchange(run(close_body, "close", [(G8 * n, HD)], s, s_before, s_after, table), n)
    return run(unpack_body, "unpack", [flat], back, leave=False).reshape(estimate.shape)


def solution(mesh):
    placed = (
        P("chan", None, "facet"),
        P("chan", None, "facet"),
        P("chan", None, "facet"),
        P(),
        P(),
        P(),
    )
    return jax.shard_map(
        per_device, mesh=mesh, in_specs=placed, out_specs=P("chan", None, "facet"), check_vma=False
    )
```

```python
import math

import jax
import jax.numpy as jnp
from jax import lax
from jax.experimental import pallas as pl
from jax.experimental.pallas import tpu as pltpu
from jax.sharding import PartitionSpec as P


OV = 16
CL = 4
WL = 2
HD = 128
G8 = CL * WL
ARRAYS = 3
F32 = jnp.float32


def lanes(shape):
    return lax.broadcasted_iota(jnp.int32, shape, 1)


def shift(x, by):
    by %= x.shape[1]
    return pltpu.roll(x, by, 1) if by else x


def pack_center(pieces, offset):
    group = lanes(pieces[0].shape) // OV
    out = shift(pieces[0], -offset)
    for g in range(1, G8):
        out = jnp.where(group == g, shift(pieces[g], OV * g - offset), out)
    return out


def pack_edges(edges, offset):
    group = lanes(edges[0].shape) // (WL * OV)
    out = shift(edges[0], -offset)
    for c in range(1, CL):
        out = jnp.where(group == c, shift(edges[c], WL * OV * c - offset), out)
    return out


def open_edges(before, after, c):
    lane = lanes(before.shape)
    step = WL * OV
    rest = jnp.where(lane < 2 * step, shift(after, step - step * c), 0.0)
    return jnp.where(lane < step, shift(before, -step * c), rest)


def open_center(before, after, g):
    lane = lanes(before.shape)
    rest = jnp.where(lane >= HD - OV, shift(after, HD - OV - OV * g), 0.0)
    return jnp.where(lane < OV, shift(before, -OV * g), rest)


def split(x):
    top = x.astype(jnp.bfloat16)
    return top, (x - top.astype(F32)).astype(jnp.bfloat16)


def product(a, b, contract=((1,), (0,))):
    dims = (contract, ((), ()))
    parts = ((a[0], b[1]), (a[1], b[0]), (a[0], b[0]))
    p, q, r = (lax.dot_general(u, v, dims, preferred_element_type=F32) for u, v in parts)
    return p + q + r


def put_gram(x, tri):
    half = x.shape[0] // 2
    parts = split(x[...])
    low, high = ([p[i * half : i * half + half, :] for p in parts] for i in (0, 1))
    rows = ((1,), (1,))
    first, second = product(low, low, rows), product(high, high, rows)
    row = lax.broadcasted_iota(jnp.int32, first.shape, 0)
    col = lanes(first.shape)
    tri[0:half, :] = product(low, high, rows)
    tri[half : 2 * half, :] = jnp.where(row >= col, first, second)
    diagonal = jnp.sum(jnp.where(row == col, second, 0.0), axis=0, keepdims=True)
    rest = (tri.shape[0] - 2 * half, half)
    tri[2 * half :, :] = jnp.where(lax.broadcasted_iota(jnp.int32, rest, 0) == 0, diagonal, 0.0)


def get_gram(tri, gram):
    half = gram.shape[0] // 2
    above, both = tri[0:half, :], tri[half : 2 * half, :]
    row = lax.broadcasted_iota(jnp.int32, both.shape, 0)
    col = lanes(both.shape)
    turned = both.T
    gram[0:half, 0:half] = jnp.where(row >= col, both, turned)
    gram[0:half, half:] = above
    gram[half:, 0:half] = above.T
    diagonal = jnp.where(row == col, tri[2 * half : 2 * half + 1, :], turned)
    gram[half:, half:] = jnp.where(row < col, both, diagonal)
    return gram[...]


def pack_body(est, dirty, weights, out):
    n = out.shape[0] // (ARRAYS * G8)
    for c in range(CL):
        for w in range(WL):
            rows = pl.ds(c * WL * n + w, n, stride=WL)
            e, d, k = est[rows, :], dirty[rows, :], weights[rows, :]
            for a, value in enumerate((e - k * (e - d), d, k)):
                out[pl.ds(a * G8 + c * WL + w, n, stride=ARRAYS * G8), :] = value


def give(low, high, even):
    return jnp.where(even, high, low), jnp.where(even, low, high)


def take(near, far, even):
    return jnp.where(even, far, near), jnp.where(even, near, far)


def piece(got, a, g):
    n = got.shape[0] // (ARRAYS * G8)
    return got[pl.ds(a * G8 + g, n, stride=ARRAYS * G8), :]


def edge_body(got, table, near, far):
    n = near.shape[0] // ARRAYS
    even = table[5:6, :HD] > 0.5
    for a in range(ARRAYS):
        pieces = [piece(got, a, g) for g in range(G8)]
        rows = pl.ds(a * n, n)
        near[rows, :], far[rows, :] = give(pack_center(pieces, 0), pack_center(pieces, HD - OV), even)


def gram_body(got, near, far, table, x, tri):
    n = near.shape[0] // ARRAYS
    even = table[5:6, :HD] > 0.5
    keep = table[0:1, WL * HD :]
    before, after = take(near[0:n, :], far[0:n, :], even)
    for c in range(CL):
        rows = pl.ds(c * n, n)
        for w in range(WL):
            x[rows, pl.ds(w * HD, HD)] = piece(got, 0, c * WL + w)
        x[rows, pl.ds(WL * HD, HD)] = open_edges(before, after, c) * keep
    put_gram(x, tri)


def shrink_of(gram, x, factor):
    count = gram.shape[0]
    row = lax.broadcasted_iota(jnp.int32, gram.shape, 0)
    identity = (row == lanes(gram.shape)).astype(F32)
    trace = jnp.sum(jnp.sum(gram * identity, axis=1, keepdims=True), axis=0, keepdims=True)
    mean_eigen = trace / count + 1e-06
    target = (gram + (0.01 * mean_eigen) * identity) / (16.16 * mean_eigen)
    first = 1.5 * identity - 0.5 * target
    first_parts = split(first)
    target = product(split(target), first_parts)
    second = 1.5 * identity - 0.5 * product(first_parts, split(target))
    inverse_root = product(split(second), first_parts)
    return product(split(identity - factor * inverse_root), split(x))


def apply_body(step, last, tri, x, table, out, near, far, gram):
    n = x.shape[0] // CL
    even = table[5:6, :HD] > 0.5
    factor = table[3 + step : 4 + step, : gram.shape[0]]
    out[...] = shrink_of(get_gram(tri, gram), x[...], factor) * table[1:2, :]
    edges = [out[pl.ds(c * n, n), pl.ds(WL * HD, HD)] for c in range(CL)]
    near[0:n, :], far[0:n, :] = give(pack_edges(edges, 0), pack_edges(edges, WL * OV), even)
    if not last:
        pieces = [out[pl.ds(c * n, n), pl.ds(w * HD, HD)] for c in range(CL) for w in range(WL)]
        rows = slice(n, 2 * n)
        near[rows, :], far[rows, :] = give(pack_center(pieces, 0), pack_center(pieces, HD - OV), even)


def next_body(got, near, far, s, s_near, s_far, table, x, tri):
    n = near.shape[0] // ARRAYS
    even = table[5:6, :HD] > 0.5
    keep = table[0:1, WL * HD :]
    scale = table[2:3, :]
    center = take(s_near[0:n, :], s_far[0:n, :], even)
    outer = take(s_near[n : 2 * n, :], s_far[n : 2 * n, :], even)
    d_edges = take(near[n : 2 * n, :], far[n : 2 * n, :], even)
    k_edges = take(near[2 * n :, :], far[2 * n :, :], even)
    for c in range(CL):
        rows = pl.ds(c * n, n)

        def moved(total, cols, d, k):
            current = total * scale[:, cols]
            return current - k * (current - d)

        for w in range(WL):
            g = c * WL + w
            cols = slice(w * HD, w * HD + HD)
            total = s[rows, cols] + open_center(*center, g)
            x[rows, cols] = moved(total, cols, piece(got, 1, g), piece(got, 2, g))
        cols = slice(WL * HD, WL * HD + HD)
        total = s[rows, cols] + open_edges(*outer, c)
        x[rows, cols] = moved(total, cols, open_edges(*d_edges, c), open_edges(*k_edges, c)) * keep
    put_gram(x, tri)


def close_body(s, near, far, table, out):
    n = near.shape[0]
    center = take(near[...], far[...], table[5:6, :HD] > 0.5)
    for c in range(CL):
        for w in range(WL):
            g = c * WL + w
            total = s[pl.ds(c * n, n), pl.ds(w * HD, HD)] + open_center(*center, g)
            out[pl.ds(g, n, stride=G8), :] = total * table[2:3, w * HD : w * HD + HD]


def unpack_body(got, out):
    n = got.shape[0] // G8
    for c in range(CL):
        for w in range(WL):
            out[pl.ds(c * WL * n + w, n, stride=WL), :] = got[pl.ds(c * WL + w, n, stride=G8), :]


def run(body, name, shapes, *args, enter=True, leave=True, scratch=()):
    spec = pl.BlockSpec(memory_space=pltpu.VMEM)
    outs = [pltpu.VMEM(s, F32) if leave else jax.ShapeDtypeStruct(s, F32) for s in shapes]
    single = len(outs) == 1
    if enter:
        args = [pltpu.with_memory_space_constraint(a, pltpu.VMEM) for a in args]
    return pl.pallas_call(
        body,
        out_shape=outs[0] if single else outs,
        in_specs=[spec] * len(args),
        out_specs=spec if single else [spec] * len(outs),
        scratch_shapes=[pltpu.VMEM(t, F32) for t in scratch],
        name=name,
    )(*args)


def exchange(x, n):
    return lax.all_to_all(x.reshape(n, -1, HD), "chan", 0, 0).reshape(x.shape)


def swap(near, far):
    size = lax.axis_size("facet")
    apart = [(i, i + 1) for i in range(1, size - 1, 2)]
    beside = [(i, i + 1) for i in range(0, size, 2)]
    near = lax.ppermute(near, "facet", beside + [(j, i) for i, j in beside])
    far = lax.ppermute(far, "facet", apart + [(j, i) for i, j in apart])
    return near, far


def total_gram(tri, n):
    parts = tri.reshape(n, 1, -1)
    mine = jnp.sum(lax.all_to_all(parts, "chan", 0, 0), axis=0, keepdims=True)
    return lax.all_to_all(jnp.broadcast_to(mine, parts.shape), "chan", 0, 0).reshape(tri.shape)


def tables(margin, blend_table, tau_steps, channels):
    facet_id = lax.axis_index("facet")
    facet_total = lax.axis_size("facet")
    row_index = jnp.arange(HD + 2 * OV, dtype=jnp.int32)[None, :]
    keep_all = (
        (row_index >= OV - margin[:, None]) & (row_index < HD + OV + margin[:, None])
    ).astype(F32)
    weight_all = blend_table.astype(F32) * keep_all
    row_weight = weight_all[facet_id]
    before = weight_all[jnp.maximum(facet_id - 1, 0)][HD:] * (facet_id > 0)
    after = weight_all[jnp.minimum(facet_id + 1, facet_total - 1)][: 2 * OV] * (
        facet_id < facet_total - 1
    )
    total = row_weight + jnp.concatenate([before, jnp.zeros((HD - 2 * OV,), F32), after])
    scale = 1.0 / jnp.where(total == 0.0, 1.0, total)
    rows = jnp.stack([keep_all[facet_id], row_weight, scale])
    center, low, high = rows[:, OV : OV + HD], rows[:, :OV], rows[:, OV + HD :]
    pad = jnp.zeros((3, HD - 4 * OV), F32)
    rows = jnp.concatenate([center, center, low, low, high, high, pad], axis=1)
    factors = 0.1 * tau_steps.astype(F32) / math.sqrt(1.01)
    factors = jnp.broadcast_to(factors[:, None], (tau_steps.shape[0], rows.shape[1]))
    even = jnp.broadcast_to((facet_id % 2 == 0).astype(F32), (1, rows.shape[1]))
    return jnp.concatenate([rows, factors, even, jnp.zeros((2, rows.shape[1]), F32)])


def per_device(estimate, dirty, weights, margin, blend_table, tau_steps):
    n = lax.axis_size("chan")
    c, width = n * CL, (WL + 1) * HD
    assert estimate.shape == (CL, n * WL, HD)
    table = tables(margin, blend_table, tau_steps, c)
    flat = (CL * WL * n, HD)
    sent = run(
        pack_body, "pack", [(ARRAYS * G8 * n, HD)], estimate.reshape(flat), dirty.reshape(flat), weights.reshape(flat), enter=False
    )
    got = exchange(sent, n)
    near, far = swap(*run(edge_body, "edges", [(ARRAYS * n, HD)] * 2, got, table))
    sums = (n * pl.cdiv(c * (c + 1) // 2, n * HD), HD)
    x, gram = run(gram_body, "gram", [(c, width), sums], got, near, far, table)
    gram = total_gram(gram, n)
    s, s_near, s_far = run(
        lambda *refs: apply_body(0, False, *refs), "shrink", [(c, width), (2 * n, HD), (2 * n, HD)], gram, x, table, scratch=[(c, c)]
    )
    s_near, s_far = swap(s_near, s_far)
    x, gram = run(next_body, "step", [(c, width), sums], got, near, far, s, s_near, s_far, table)
    gram = total_gram(gram, n)
    s, s_near, s_far = run(
        lambda *refs: apply_body(1, True, *refs), "last", [(c, width), (n, HD), (n, HD)], gram, x, table, scratch=[(c, c)]
    )
    s_near, s_far = swap(s_near, s_far)
    back = exchange(run(close_body, "close", [(G8 * n, HD)], s, s_near, s_far, table), n)
    return run(unpack_body, "unpack", [flat], back, leave=False).reshape(estimate.shape)


def solution(mesh):
    placed = (
        P("chan", None, "facet"),
        P("chan", None, "facet"),
        P("chan", None, "facet"),
        P(),
        P(),
        P(),
    )
    return jax.shard_map(
        per_device, mesh=mesh, in_specs=placed, out_specs=P("chan", None, "facet"), check_vma=False
    )
```

```python
import math

import jax
import jax.numpy as jnp
from jax import lax
from jax.experimental import pallas as pl
from jax.experimental.pallas import tpu as pltpu
from jax.sharding import PartitionSpec as P


OV = 16
CL = 4
WL = 2
HD = 128
G8 = CL * WL
ARRAYS = 3
F32 = jnp.float32


def lanes(shape):
    return lax.broadcasted_iota(jnp.int32, shape, 1)


def shift(x, by):
    by %= x.shape[1]
    return pltpu.roll(x, by, 1) if by else x


def pack_center(pieces, offset):
    group = lanes(pieces[0].shape) // OV
    out = shift(pieces[0], -offset)
    for g in range(1, G8):
        out = jnp.where(group == g, shift(pieces[g], OV * g - offset), out)
    return out


def pack_edges(edges, offset):
    group = lanes(edges[0].shape) // (WL * OV)
    out = shift(edges[0], -offset)
    for c in range(1, CL):
        out = jnp.where(group == c, shift(edges[c], WL * OV * c - offset), out)
    return out


def open_edges(before, after, c):
    lane = lanes(before.shape)
    step = WL * OV
    rest = jnp.where(lane < 2 * step, shift(after, step - step * c), 0.0)
    return jnp.where(lane < step, shift(before, -step * c), rest)


def open_center(before, after, g):
    lane = lanes(before.shape)
    rest = jnp.where(lane >= HD - OV, shift(after, HD - OV - OV * g), 0.0)
    return jnp.where(lane < OV, shift(before, -OV * g), rest)


def split(x):
    top = x.astype(jnp.bfloat16)
    return top, (x - top.astype(F32)).astype(jnp.bfloat16)


def product(a, b, contract=((1,), (0,))):
    dims = (contract, ((), ()))
    parts = ((a[0], b[1]), (a[1], b[0]), (a[0], b[0]))
    p, q, r = (lax.dot_general(u, v, dims, preferred_element_type=F32) for u, v in parts)
    return p + q + r


def put_gram(x, tri):
    half = x.shape[0] // 2
    parts = split(x[...])
    low, high = ([p[i * half : i * half + half, :] for p in parts] for i in (0, 1))
    rows = ((1,), (1,))
    first, second = product(low, low, rows), product(high, high, rows)
    row = lax.broadcasted_iota(jnp.int32, first.shape, 0)
    col = lanes(first.shape)
    tri[0:half, :] = product(low, high, rows)
    tri[half : 2 * half, :] = jnp.where(row >= col, first, second)
    diagonal = jnp.sum(jnp.where(row == col, second, 0.0), axis=0, keepdims=True)
    rest = (tri.shape[0] - 2 * half, half)
    tri[2 * half :, :] = jnp.where(lax.broadcasted_iota(jnp.int32, rest, 0) == 0, diagonal, 0.0)


def get_gram(tri, gram):
    half = gram.shape[0] // 2
    above, both = tri[0:half, :], tri[half : 2 * half, :]
    row = lax.broadcasted_iota(jnp.int32, both.shape, 0)
    col = lanes(both.shape)
    turned = both.T
    gram[0:half, 0:half] = jnp.where(row >= col, both, turned)
    gram[0:half, half:] = above
    gram[half:, 0:half] = above.T
    diagonal = jnp.where(row == col, tri[2 * half : 2 * half + 1, :], turned)
    gram[half:, half:] = jnp.where(row < col, both, diagonal)
    return gram[...]


def pack_body(est, dirty, weights, out):
    n = out.shape[0] // (ARRAYS * G8)
    for c in range(CL):
        for w in range(WL):
            rows = pl.ds(c * WL * n + w, n, stride=WL)
            e, d, k = est[rows, :], dirty[rows, :], weights[rows, :]
            for a, value in enumerate((e - k * (e - d), d, k)):
                out[pl.ds(a * G8 + c * WL + w, n, stride=ARRAYS * G8), :] = value


def give(low, high, even):
    return jnp.where(even, high, low), jnp.where(even, low, high)


def take(near, far, even):
    return jnp.where(even, far, near), jnp.where(even, near, far)


def piece(got, a, g):
    n = got.shape[0] // (ARRAYS * G8)
    return got[pl.ds(a * G8 + g, n, stride=ARRAYS * G8), :]


def edge_body(got, table, near, far):
    n = near.shape[0] // ARRAYS
    even = table[5:6, :HD] > 0.5
    for a in range(ARRAYS):
        pieces = [piece(got, a, g) for g in range(G8)]
        rows = pl.ds(a * n, n)
        near[rows, :], far[rows, :] = give(pack_center(pieces, 0), pack_center(pieces, HD - OV), even)


def gram_body(got, near, far, table, x, tri):
    n = near.shape[0] // ARRAYS
    even = table[5:6, :HD] > 0.5
    keep = table[0:1, WL * HD :]
    before, after = take(near[0:n, :], far[0:n, :], even)
    for c in range(CL):
        rows = pl.ds(c * n, n)
        for w in range(WL):
            x[rows, pl.ds(w * HD, HD)] = piece(got, 0, c * WL + w)
        x[rows, pl.ds(WL * HD, HD)] = open_edges(before, after, c) * keep
    put_gram(x, tri)


def shrink_of(gram, x, factor):
    count = gram.shape[0]
    row = lax.broadcasted_iota(jnp.int32, gram.shape, 0)
    identity = (row == lanes(gram.shape)).astype(F32)
    trace = jnp.sum(jnp.sum(gram * identity, axis=1, keepdims=True), axis=0, keepdims=True)
    mean_eigen = trace / count + 1e-06
    target = (gram + (0.01 * mean_eigen) * identity) / (16.16 * mean_eigen)
    first = 1.5 * identity - 0.5 * target
    first_parts = split(first)
    target = product(split(target), first_parts)
    second = 1.5 * identity - 0.5 * product(first_parts, split(target))
    inverse_root = product(split(second), first_parts)
    return product(split(identity - factor * inverse_root), split(x))


def apply_body(step, last, tri, x, table, out, near, far, gram):
    n = x.shape[0] // CL
    even = table[5:6, :HD] > 0.5
    factor = table[3 + step : 4 + step, : gram.shape[0]]
    out[...] = shrink_of(get_gram(tri, gram), x[...], factor) * table[1:2, :]
    edges = [out[pl.ds(c * n, n), pl.ds(WL * HD, HD)] for c in range(CL)]
    near[0:n, :], far[0:n, :] = give(pack_edges(edges, 0), pack_edges(edges, WL * OV), even)
    if not last:
        pieces = [out[pl.ds(c * n, n), pl.ds(w * HD, HD)] for c in range(CL) for w in range(WL)]
        rows = slice(n, 2 * n)
        near[rows, :], far[rows, :] = give(pack_center(pieces, 0), pack_center(pieces, HD - OV), even)


def next_body(got, near, far, s, s_near, s_far, table, x, tri):
    n = near.shape[0] // ARRAYS
    even = table[5:6, :HD] > 0.5
    keep = table[0:1, WL * HD :]
    scale = table[2:3, :]
    center = take(s_near[0:n, :], s_far[0:n, :], even)
    outer = take(s_near[n : 2 * n, :], s_far[n : 2 * n, :], even)
    d_edges = take(near[n : 2 * n, :], far[n : 2 * n, :], even)
    k_edges = take(near[2 * n :, :], far[2 * n :, :], even)
    for c in range(CL):
        rows = pl.ds(c * n, n)

        def moved(total, cols, d, k):
            current = total * scale[:, cols]
            return current - k * (current - d)

        for w in range(WL):
            g = c * WL + w
            cols = slice(w * HD, w * HD + HD)
            total = s[rows, cols] + open_center(*center, g)
            x[rows, cols] = moved(total, cols, piece(got, 1, g), piece(got, 2, g))
        cols = slice(WL * HD, WL * HD + HD)
        total = s[rows, cols] + open_edges(*outer, c)
        x[rows, cols] = moved(total, cols, open_edges(*d_edges, c), open_edges(*k_edges, c)) * keep
    put_gram(x, tri)


def close_body(s, near, far, table, out):
    n = near.shape[0]
    center = take(near[...], far[...], table[5:6, :HD] > 0.5)
    for c in range(CL):
        for w in range(WL):
            g = c * WL + w
            total = s[pl.ds(c * n, n), pl.ds(w * HD, HD)] + open_center(*center, g)
            out[pl.ds(g, n, stride=G8), :] = total * table[2:3, w * HD : w * HD + HD]


def unpack_body(got, out):
    n = got.shape[0] // G8
    for c in range(CL):
        for w in range(WL):
            out[pl.ds(c * WL * n + w, n, stride=WL), :] = got[pl.ds(c * WL + w, n, stride=G8), :]


def run(body, shapes, *args, enter=True, leave=True, scratch=()):
    spec = pl.BlockSpec(memory_space=pltpu.VMEM)
    outs = [pltpu.VMEM(s, F32) if leave else jax.ShapeDtypeStruct(s, F32) for s in shapes]
    single = len(outs) == 1
    if enter:
        args = [pltpu.with_memory_space_constraint(a, pltpu.VMEM) for a in args]
    return pl.pallas_call(
        body,
        out_shape=outs[0] if single else outs,
        in_specs=[spec] * len(args),
        out_specs=spec if single else [spec] * len(outs),
        scratch_shapes=[pltpu.VMEM(t, F32) for t in scratch],
    )(*args)


def exchange(x, n):
    return lax.all_to_all(x.reshape(n, -1, HD), "chan", 0, 0).reshape(x.shape)


def swap(near, far):
    size = lax.axis_size("facet")
    apart = [(i, i + 1) for i in range(1, size - 1, 2)]
    beside = [(i, i + 1) for i in range(0, size, 2)]
    near = lax.ppermute(near, "facet", beside + [(j, i) for i, j in beside])
    far = lax.ppermute(far, "facet", apart + [(j, i) for i, j in apart])
    return near, far


def total_gram(tri, n):
    parts = tri.reshape(n, 1, -1)
    mine = jnp.sum(lax.all_to_all(parts, "chan", 0, 0), axis=0, keepdims=True)
    return lax.all_to_all(jnp.broadcast_to(mine, parts.shape), "chan", 0, 0).reshape(tri.shape)


def tables(margin, blend_table, tau_steps):
    facet_id = lax.axis_index("facet")
    facet_total = lax.axis_size("facet")
    row_index = jnp.arange(HD + 2 * OV, dtype=jnp.int32)[None, :]
    keep_all = (
        (row_index >= OV - margin[:, None]) & (row_index < HD + OV + margin[:, None])
    ).astype(F32)
    weight_all = blend_table.astype(F32) * keep_all
    row_weight = weight_all[facet_id]
    before = weight_all[jnp.maximum(facet_id - 1, 0)][HD:] * (facet_id > 0)
    after = weight_all[jnp.minimum(facet_id + 1, facet_total - 1)][: 2 * OV] * (
        facet_id < facet_total - 1
    )
    total = row_weight + jnp.concatenate([before, jnp.zeros((HD - 2 * OV,), F32), after])
    scale = 1.0 / jnp.where(total == 0.0, 1.0, total)
    rows = jnp.stack([keep_all[facet_id], row_weight, scale])
    center, low, high = rows[:, OV : OV + HD], rows[:, :OV], rows[:, OV + HD :]
    pad = jnp.zeros((3, HD - 4 * OV), F32)
    rows = jnp.concatenate([center, center, low, low, high, high, pad], axis=1)
    factors = 0.1 * tau_steps.astype(F32) / math.sqrt(1.01)
    factors = jnp.broadcast_to(factors[:, None], (tau_steps.shape[0], rows.shape[1]))
    even = jnp.broadcast_to((facet_id % 2 == 0).astype(F32), (1, rows.shape[1]))
    return jnp.concatenate([rows, factors, even, jnp.zeros((2, rows.shape[1]), F32)])


def per_device(estimate, dirty, weights, margin, blend_table, tau_steps):
    n = lax.axis_size("chan")
    c, width = n * CL, (WL + 1) * HD
    assert estimate.shape == (CL, n * WL, HD)
    table = tables(margin, blend_table, tau_steps)
    flat = (CL * WL * n, HD)
    sent = run(
        pack_body, [(ARRAYS * G8 * n, HD)], estimate.reshape(flat), dirty.reshape(flat), weights.reshape(flat), enter=False
    )
    got = exchange(sent, n)
    near, far = swap(*run(edge_body, [(ARRAYS * n, HD)] * 2, got, table))
    sums = (n * pl.cdiv(c * (c + 1) // 2, n * HD), HD)
    x, gram = run(gram_body, [(c, width), sums], got, near, far, table)
    gram = total_gram(gram, n)
    s, s_near, s_far = run(
        lambda *refs: apply_body(0, False, *refs), [(c, width), (2 * n, HD), (2 * n, HD)], gram, x, table, scratch=[(c, c)]
    )
    s_near, s_far = swap(s_near, s_far)
    x, gram = run(next_body, [(c, width), sums], got, near, far, s, s_near, s_far, table)
    gram = total_gram(gram, n)
    s, s_near, s_far = run(
        lambda *refs: apply_body(1, True, *refs), [(c, width), (n, HD), (n, HD)], gram, x, table, scratch=[(c, c)]
    )
    s_near, s_far = swap(s_near, s_far)
    back = exchange(run(close_body, [(G8 * n, HD)], s, s_near, s_far, table), n)
    return run(unpack_body, [flat], back, leave=False).reshape(estimate.shape)


def solution(mesh):
    placed = (
        P("chan", None, "facet"),
        P("chan", None, "facet"),
        P("chan", None, "facet"),
        P(),
        P(),
        P(),
    )

    return jax.shard_map(per_device, mesh=mesh, in_specs=placed, out_specs=P("chan", None, "facet"), check_vma=False)
```

```python
import math

import jax
import jax.numpy as jnp
from jax import lax
from jax.experimental import pallas as pl
from jax.experimental.pallas import tpu as pltpu
from jax.sharding import PartitionSpec as P


OV = 16
CL = 4
WL = 2
HD = 128
G8 = CL * WL
ARRAYS = 3
F32 = jnp.float32


def lanes(shape):
    return lax.broadcasted_iota(jnp.int32, shape, 1)


def shift(x, by):
    by %= x.shape[1]
    return pltpu.roll(x, by, 1) if by else x


def pack_center(pieces, offset):
    group = lanes(pieces[0].shape) // OV
    out = shift(pieces[0], -offset)
    for g in range(1, G8):
        out = jnp.where(group == g, shift(pieces[g], OV * g - offset), out)
    return out


def pack_edges(edges, offset):
    group = lanes(edges[0].shape) // (WL * OV)
    out = shift(edges[0], -offset)
    for c in range(1, CL):
        out = jnp.where(group == c, shift(edges[c], WL * OV * c - offset), out)
    return out


def open_edges(before, after, c):
    lane = lanes(before.shape)
    step = WL * OV
    rest = jnp.where(lane < 2 * step, shift(after, step - step * c), 0.0)
    return jnp.where(lane < step, shift(before, -step * c), rest)


def open_center(before, after, g):
    lane = lanes(before.shape)
    rest = jnp.where(lane >= HD - OV, shift(after, HD - OV - OV * g), 0.0)
    return jnp.where(lane < OV, shift(before, -OV * g), rest)


def split(x):
    top = x.astype(jnp.bfloat16)
    return top, (x - top.astype(F32)).astype(jnp.bfloat16)


def product(a, b, contract=((1,), (0,))):
    dims = (contract, ((), ()))
    parts = ((a[0], b[1]), (a[1], b[0]), (a[0], b[0]))
    p, q, r = (lax.dot_general(u, v, dims, preferred_element_type=F32) for u, v in parts)
    return p + q + r


def put_gram(x, tri):
    half = x.shape[0] // 2
    parts = split(x[...])
    low, high = ([p[i * half : i * half + half, :] for p in parts] for i in (0, 1))
    rows = ((1,), (1,))
    first, second = product(low, low, rows), product(high, high, rows)
    row = lax.broadcasted_iota(jnp.int32, first.shape, 0)
    col = lanes(first.shape)
    tri[0:half, :] = product(low, high, rows)
    tri[half : 2 * half, :] = jnp.where(row >= col, first, second)
    diagonal = jnp.sum(jnp.where(row == col, second, 0.0), axis=0, keepdims=True)
    rest = (tri.shape[0] - 2 * half, half)
    tri[2 * half :, :] = jnp.where(lax.broadcasted_iota(jnp.int32, rest, 0) == 0, diagonal, 0.0)


def get_gram(tri, gram):
    half = gram.shape[0] // 2
    above, both = tri[0:half, :], tri[half : 2 * half, :]
    row = lax.broadcasted_iota(jnp.int32, both.shape, 0)
    col = lanes(both.shape)
    turned = both.T
    gram[0:half, 0:half] = jnp.where(row >= col, both, turned)
    gram[0:half, half:] = above
    gram[half:, 0:half] = above.T
    diagonal = jnp.where(row == col, tri[2 * half : 2 * half + 1, :], turned)
    gram[half:, half:] = jnp.where(row < col, both, diagonal)
    return gram[...]


def pack_body(est, dirty, weights, out):
    n = out.shape[0] // (ARRAYS * G8)
    for c in range(CL):
        for w in range(WL):
            rows = pl.ds(c * WL * n + w, n, stride=WL)
            e, d, k = est[rows, :], dirty[rows, :], weights[rows, :]
            for a, value in enumerate((e - k * (e - d), d, k)):
                out[pl.ds(a * G8 + c * WL + w, n, stride=ARRAYS * G8), :] = value


def is_even():
    return lax.axis_index("facet") % 2 == 0


def give(low, high):
    even = is_even()
    return jnp.where(even, high, low), jnp.where(even, low, high)


def take(near, far):
    even = is_even()
    return jnp.where(even, far, near), jnp.where(even, near, far)


def piece(got, a, g):
    n = got.shape[0] // (ARRAYS * G8)
    return got[pl.ds(a * G8 + g, n, stride=ARRAYS * G8), :]


def edge_body(got, near, far):
    n = near.shape[0] // 2
    for i, a in enumerate((0, 2)):
        pieces = [piece(got, a, g) for g in range(G8)]
        rows = pl.ds(i * n, n)
        near[rows, :], far[rows, :] = give(pack_center(pieces, 0), pack_center(pieces, HD - OV))


def gram_body(got, near, far, table, x, tri):
    n = near.shape[0] // 2
    keep = table[0:1, WL * HD :]
    before, after = take(near[0:n, :], far[0:n, :])
    for c in range(CL):
        rows = pl.ds(c * n, n)
        for w in range(WL):
            x[rows, pl.ds(w * HD, HD)] = piece(got, 0, c * WL + w)
        x[rows, pl.ds(WL * HD, HD)] = open_edges(before, after, c) * keep
    put_gram(x, tri)


def shrink_of(gram, x, factor):
    count = gram.shape[0]
    row = lax.broadcasted_iota(jnp.int32, gram.shape, 0)
    identity = (row == lanes(gram.shape)).astype(F32)
    trace = jnp.sum(jnp.sum(gram * identity, axis=1, keepdims=True), axis=0, keepdims=True)
    mean_eigen = trace / count + 1e-06
    target = (gram + (0.01 * mean_eigen) * identity) / (16.16 * mean_eigen)
    first = 1.5 * identity - 0.5 * target
    parts = split(target)
    square = product(parts, parts)
    stepped = 1.5 * target - 0.5 * square
    twice = 2.25 * identity - 1.5 * target + 0.25 * square
    inverse_root = 1.5 * first - 0.5 * product(split(stepped), split(twice))
    return product(split(identity - factor * inverse_root), split(x))


def apply_body(step, tri, x, table, out, near, far, gram):
    n = x.shape[0] // CL
    factor = table[3 + step : 4 + step, : gram.shape[0]]
    out[...] = shrink_of(get_gram(tri, gram), x[...], factor) * table[1:2, :]
    edges = [out[pl.ds(c * n, n), pl.ds(WL * HD, HD)] for c in range(CL)]
    near[0:n, :], far[0:n, :] = give(pack_edges(edges, 0), pack_edges(edges, WL * OV))


def zone_body(tri, x, got, table, out, near, far, gram):
    apply_body(0, tri, x, table, out, near, far, gram)
    n = x.shape[0] // CL
    pieces = []
    for g in range(G8):
        cols = pl.ds(g % WL * HD, HD)
        d, k = piece(got, 1, g), piece(got, 2, g)
        own = out[pl.ds(g // WL * n, n), cols] * table[2:3, :HD]
        pieces.append(own - k * (own - d))
    rows = slice(n, 2 * n)
    near[rows, :], far[rows, :] = give(pack_center(pieces, 0), pack_center(pieces, HD - OV))


def next_body(got, near, far, s, s_near, s_far, table, x, tri):
    n = near.shape[0] // 2
    keep = table[0:1, WL * HD :]
    scale = table[2:3, :]
    center = take(s_near[0:n, :], s_far[0:n, :])
    outer = take(s_near[n : 2 * n, :], s_far[n : 2 * n, :])
    k_edges = take(near[n : 2 * n, :], far[n : 2 * n, :])
    for c in range(CL):
        rows = pl.ds(c * n, n)
        for w in range(WL):
            g = c * WL + w
            cols = slice(w * HD, w * HD + HD)
            d, k = piece(got, 1, g), piece(got, 2, g)
            current = (s[rows, cols] + open_center(*center, g)) * scale[:, cols]
            x[rows, cols] = current - k * (current - d)
        cols = slice(WL * HD, WL * HD + HD)
        own = s[rows, cols] * scale[:, cols]
        x[rows, cols] = (own - open_edges(*k_edges, c) * own + open_edges(*outer, c)) * keep
    put_gram(x, tri)


def close_body(s, near, far, table, out):
    n = near.shape[0]
    center = take(near[...], far[...])
    for c in range(CL):
        for w in range(WL):
            g = c * WL + w
            total = s[pl.ds(c * n, n), pl.ds(w * HD, HD)] + open_center(*center, g)
            out[pl.ds(g, n, stride=G8), :] = total * table[2:3, w * HD : w * HD + HD]


def unpack_body(got, out):
    n = got.shape[0] // G8
    for c in range(CL):
        for w in range(WL):
            out[pl.ds(c * WL * n + w, n, stride=WL), :] = got[pl.ds(c * WL + w, n, stride=G8), :]


def run(body, shapes, *args, enter=True, leave=True, scratch=()):
    spec = pl.BlockSpec(memory_space=pltpu.VMEM)
    outs = [pltpu.VMEM(s, F32) if leave else jax.ShapeDtypeStruct(s, F32) for s in shapes]
    single = len(outs) == 1
    if enter:
        args = [pltpu.with_memory_space_constraint(a, pltpu.VMEM) for a in args]
    return pl.pallas_call(
        body,
        out_shape=outs[0] if single else outs,
        in_specs=[spec] * len(args),
        out_specs=spec if single else [spec] * len(outs),
        scratch_shapes=[pltpu.VMEM(t, F32) for t in scratch],
    )(*args)


def exchange(x, n):
    return lax.all_to_all(x.reshape(n, -1, HD), "chan", 0, 0).reshape(x.shape)


def swap(near, far):
    size = lax.axis_size("facet")
    apart = [(i, i + 1) for i in range(1, size - 1, 2)]
    beside = [(i, i + 1) for i in range(0, size, 2)]
    near = lax.ppermute(near, "facet", beside + [(j, i) for i, j in beside])
    far = lax.ppermute(far, "facet", apart + [(j, i) for i, j in apart])
    return near, far


def total_gram(tri, n):
    parts = tri.reshape(n, 1, -1)
    mine = jnp.sum(lax.all_to_all(parts, "chan", 0, 0), axis=0, keepdims=True)
    return lax.all_to_all(jnp.broadcast_to(mine, parts.shape), "chan", 0, 0).reshape(tri.shape)


def tables(margin, blend_table, tau_steps):
    facet_id = lax.axis_index("facet")
    facet_total = lax.axis_size("facet")
    row_index = jnp.arange(HD + 2 * OV, dtype=jnp.int32)[None, :]
    keep_all = (
        (row_index >= OV - margin[:, None]) & (row_index < HD + OV + margin[:, None])
    ).astype(F32)
    weight_all = blend_table.astype(F32) * keep_all
    row_weight = weight_all[facet_id]
    before = weight_all[:, HD:][jnp.maximum(facet_id - 1, 0)] * (facet_id > 0)
    after = weight_all[:, : 2 * OV][jnp.minimum(facet_id + 1, facet_total - 1)] * (
        facet_id < facet_total - 1
    )
    total = row_weight + jnp.pad(before, (0, HD)) + jnp.pad(after, (HD, 0))
    scale = 1.0 / jnp.where(total == 0.0, 1.0, total)
    rows = jnp.stack([keep_all[facet_id], row_weight, scale])
    center, low, high = rows[:, OV : OV + HD], rows[:, :OV], rows[:, OV + HD :]
    rows = jnp.concatenate([center, center, low, low, high, high], axis=1)
    rows = jnp.pad(rows, ((0, 5), (0, HD - 4 * OV)))
    factors = 0.1 * tau_steps.astype(F32) / math.sqrt(1.01)
    return rows + jnp.pad(factors, (3, 5 - tau_steps.shape[0]))[:, None]


def per_device(estimate, dirty, weights, margin, blend_table, tau_steps):
    n = lax.axis_size("chan")
    c, width = n * CL, (WL + 1) * HD
    assert estimate.shape == (CL, n * WL, HD)
    flat = (CL * WL * n, HD)
    sent = run(
        pack_body,
        [(ARRAYS * G8 * n, HD)],
        estimate.reshape(flat),
        dirty.reshape(flat),
        weights.reshape(flat),
        enter=False,
    )
    got = exchange(sent, n)
    near, far = run(edge_body, [(2 * n, HD)] * 2, got)
    near, far, *small = lax.optimization_barrier((near, far, margin, blend_table, tau_steps))
    near, far = swap(near, far)
    table = tables(*small)
    sums = (n * pl.cdiv(c * (c + 1) // 2, n * HD), HD)
    x, gram = run(gram_body, [(c, width), sums], got, near, far, table)
    gram = total_gram(gram, n)
    s, s_near, s_far = run(
        zone_body, [(c, width), (2 * n, HD), (2 * n, HD)], gram, x, got, table, scratch=[(c, c)]
    )
    s_near, s_far = swap(s_near, s_far)
    x, gram = run(next_body, [(c, width), sums], got, near, far, s, s_near, s_far, table)
    gram = total_gram(gram, n)
    s, s_near, s_far = run(
        lambda *refs: apply_body(1, *refs), [(c, width), (n, HD), (n, HD)], gram, x, table, scratch=[(c, c)]
    )
    s_near, s_far = swap(s_near, s_far)
    back = exchange(run(close_body, [(G8 * n, HD)], s, s_near, s_far, table), n)
    return run(unpack_body, [flat], back, leave=False).reshape(estimate.shape)


def solution(mesh):
    placed = (
        P("chan", None, "facet"),
        P("chan", None, "facet"),
        P("chan", None, "facet"),
        P(),
        P(),
        P(),
    )

    return jax.shard_map(per_device, mesh=mesh, in_specs=placed, out_specs=P("chan", None, "facet"), check_vma=False)
```

```python
import math

import jax
import jax.numpy as jnp
from jax import lax
from jax.experimental import pallas as pl
from jax.experimental.pallas import tpu as pltpu
from jax.sharding import PartitionSpec as P


OV = 16
CL = 4
WL = 2
HD = 128
G8 = CL * WL
ARRAYS = 3
F32 = jnp.float32


def lanes(shape):
    return lax.broadcasted_iota(jnp.int32, shape, 1)


def shift(x, by):
    by %= x.shape[1]
    return pltpu.roll(x, by, 1) if by else x


def pack_center(pieces, offset):
    group = lanes(pieces[0].shape) // OV
    out = shift(pieces[0], -offset)
    for g in range(1, G8):
        out = jnp.where(group == g, shift(pieces[g], OV * g - offset), out)
    return out


def pack_edges(edges, offset):
    group = lanes(edges[0].shape) // (WL * OV)
    out = shift(edges[0], -offset)
    for c in range(1, CL):
        out = jnp.where(group == c, shift(edges[c], WL * OV * c - offset), out)
    return out


def open_edges(before, after, c):
    lane = lanes(before.shape)
    step = WL * OV
    rest = jnp.where(lane < 2 * step, shift(after, step - step * c), 0.0)
    return jnp.where(lane < step, shift(before, -step * c), rest)


def open_center(before, after, g):
    lane = lanes(before.shape)
    rest = jnp.where(lane >= HD - OV, shift(after, HD - OV - OV * g), 0.0)
    return jnp.where(lane < OV, shift(before, -OV * g), rest)


def split(x):
    top = x.astype(jnp.bfloat16)
    return top, (x - top.astype(F32)).astype(jnp.bfloat16)


def product(a, b, contract=((1,), (0,))):
    dims = (contract, ((), ()))
    parts = ((a[0], b[1]), (a[1], b[0]), (a[0], b[0]))
    p, q, r = (lax.dot_general(u, v, dims, preferred_element_type=F32) for u, v in parts)
    return p + q + r


def put_gram(x, tri):
    half = x.shape[0] // 2
    parts = split(x[...])
    low, high = ([p[i * half : i * half + half, :] for p in parts] for i in (0, 1))
    rows = ((1,), (1,))
    first, second = product(low, low, rows), product(high, high, rows)
    row = lax.broadcasted_iota(jnp.int32, first.shape, 0)
    col = lanes(first.shape)
    tri[0:half, :] = product(low, high, rows)
    tri[half : 2 * half, :] = jnp.where(row >= col, first, second)
    diagonal = jnp.sum(jnp.where(row == col, second, 0.0), axis=0, keepdims=True)
    rest = (tri.shape[0] - 2 * half, half)
    tri[2 * half :, :] = jnp.where(lax.broadcasted_iota(jnp.int32, rest, 0) == 0, diagonal, 0.0)


def get_gram(tri, gram):
    half = gram.shape[0] // 2
    above, both = tri[0:half, :], tri[half : 2 * half, :]
    row = lax.broadcasted_iota(jnp.int32, both.shape, 0)
    col = lanes(both.shape)
    turned = both.T
    gram[0:half, 0:half] = jnp.where(row >= col, both, turned)
    gram[0:half, half:] = above
    gram[half:, 0:half] = above.T
    diagonal = jnp.where(row == col, tri[2 * half : 2 * half + 1, :], turned)
    gram[half:, half:] = jnp.where(row < col, both, diagonal)
    return gram[...]


def pack_body(est, dirty, weights, margin, blend, tau, out, margin_out, blend_out, tau_out, buf, sems, small):
    n = out.shape[0] // (ARRAYS * G8)
    copies = []
    for c in range(CL):
        rows = pl.ds(c * WL * n, WL * n)
        for a, ref in enumerate((est, dirty, weights)):
            copies.append(pltpu.make_async_copy(ref.at[rows, :], buf.at[a, rows, :], sems.at[a, c]))
            copies[-1].start()
    for i, pair in enumerate(((margin, margin_out), (blend, blend_out), (tau, tau_out))):
        copies.append(pltpu.make_async_copy(*pair, small.at[i]))
        copies[-1].start()
    for c in range(CL):
        for a in range(ARRAYS):
            copies[c * ARRAYS + a].wait()
        for w in range(WL):
            rows = pl.ds(c * WL * n + w, n, stride=WL)
            e, d, k = buf[0, rows, :], buf[1, rows, :], buf[2, rows, :]
            for a, value in enumerate((e - k * (e - d), d, k)):
                out[pl.ds(a * G8 + c * WL + w, n, stride=ARRAYS * G8), :] = value
    for copy in copies[CL * ARRAYS :]:
        copy.wait()


def is_even():
    return lax.axis_index("facet") % 2 == 0


def give(low, high):
    even = is_even()
    return jnp.where(even, high, low), jnp.where(even, low, high)


def take(near, far):
    even = is_even()
    return jnp.where(even, far, near), jnp.where(even, near, far)


def piece(got, a, g):
    n = got.shape[0] // (ARRAYS * G8)
    return got[pl.ds(a * G8 + g, n, stride=ARRAYS * G8), :]


def edge_body(got, near, far):
    n = near.shape[0] // 2
    for i, a in enumerate((0, 2)):
        pieces = [piece(got, a, g) for g in range(G8)]
        rows = pl.ds(i * n, n)
        near[rows, :], far[rows, :] = give(pack_center(pieces, 0), pack_center(pieces, HD - OV))


def gram_body(got, near, far, table, x, tri):
    n = near.shape[0] // 2
    keep = table[0:1, WL * HD :]
    before, after = take(near[0:n, :], far[0:n, :])
    for c in range(CL):
        rows = pl.ds(c * n, n)
        for w in range(WL):
            x[rows, pl.ds(w * HD, HD)] = piece(got, 0, c * WL + w)
        x[rows, pl.ds(WL * HD, HD)] = open_edges(before, after, c) * keep
    put_gram(x, tri)


def kernel_of(gram, factor):
    count = gram.shape[0]
    row = lax.broadcasted_iota(jnp.int32, gram.shape, 0)
    identity = (row == lanes(gram.shape)).astype(F32)
    trace = jnp.sum(jnp.sum(gram * identity, axis=1, keepdims=True), axis=0, keepdims=True)
    mean_eigen = trace / count + 1e-06
    target = (gram + (0.01 * mean_eigen) * identity) / (16.16 * mean_eigen)
    first = 1.5 * identity - 0.5 * target
    parts = split(target)
    square = product(parts, parts)
    stepped = 1.5 * target - 0.5 * square
    twice = 2.25 * identity - 1.5 * target + 0.25 * square
    inverse_root = 1.5 * first - 0.5 * product(split(stepped), split(twice))
    return identity - factor * inverse_root


def put_rims(edges, n, near, far):
    edges = [edges[pl.ds(c * n, n), :] for c in range(CL)]
    near[0:n, :], far[0:n, :] = give(pack_edges(edges, 0), pack_edges(edges, WL * OV))


def zone_body(tri, x, got, table, out, near, far, gram):
    n = x.shape[0] // CL
    kernel = kernel_of(get_gram(tri, gram), table[3:4, : gram.shape[0]])
    out[...] = product(split(kernel), split(x[...])) * table[1:2, :]
    put_rims(out.at[:, pl.ds(WL * HD, HD)], n, near, far)
    pieces = []
    for g in range(G8):
        cols = pl.ds(g % WL * HD, HD)
        d, k = piece(got, 1, g), piece(got, 2, g)
        own = out[pl.ds(g // WL * n, n), cols] * table[2:3, :HD]
        pieces.append(own - k * (own - d))
    rows = slice(n, 2 * n)
    near[rows, :], far[rows, :] = give(pack_center(pieces, 0), pack_center(pieces, HD - OV))


def next_body(got, near, far, s, s_near, s_far, table, x, tri):
    n = near.shape[0] // 2
    keep = table[0:1, WL * HD :]
    scale = table[2:3, :]
    center = take(s_near[0:n, :], s_far[0:n, :])
    outer = take(s_near[n : 2 * n, :], s_far[n : 2 * n, :])
    k_edges = take(near[n : 2 * n, :], far[n : 2 * n, :])
    for c in range(CL):
        rows = pl.ds(c * n, n)
        for w in range(WL):
            g = c * WL + w
            cols = slice(w * HD, w * HD + HD)
            d, k = piece(got, 1, g), piece(got, 2, g)
            current = (s[rows, cols] + open_center(*center, g)) * scale[:, cols]
            x[rows, cols] = current - k * (current - d)
        cols = slice(WL * HD, WL * HD + HD)
        own = s[rows, cols] * scale[:, cols]
        x[rows, cols] = (own - open_edges(*k_edges, c) * own + open_edges(*outer, c)) * keep
    put_gram(x, tri)


def last_body(tri, x, table, kernel, near, far, gram, edges):
    kernel[...] = kernel_of(get_gram(tri, gram), table[4:5, : gram.shape[0]])
    edges[...] = product(split(kernel[...]), split(x[:, WL * HD :])) * table[1:2, WL * HD :]
    put_rims(edges, x.shape[0] // CL, near, far)


def center_body(kernel, x, table, out):
    out[...] = product(split(kernel[...]), split(x[:, : WL * HD])) * table[1:2, : WL * HD]


def close_body(s, near, far, table, out):
    n = near.shape[0]
    center = take(near[...], far[...])
    for c in range(CL):
        for w in range(WL):
            g = c * WL + w
            total = s[pl.ds(c * n, n), pl.ds(w * HD, HD)] + open_center(*center, g)
            out[pl.ds(g, n, stride=G8), :] = total * table[2:3, w * HD : w * HD + HD]


def unpack_body(got, out):
    n = got.shape[0] // G8
    for c in range(CL):
        for w in range(WL):
            out[pl.ds(c * WL * n + w, n, stride=WL), :] = got[pl.ds(c * WL + w, n, stride=G8), :]


def run(body, shapes, *args, leave=True, scratch=()):
    spec = pl.BlockSpec(memory_space=pltpu.VMEM)
    outs = [pltpu.VMEM(s, F32) if leave else jax.ShapeDtypeStruct(s, F32) for s in shapes]
    single = len(outs) == 1
    args = [pltpu.with_memory_space_constraint(a, pltpu.VMEM) for a in args]
    return pl.pallas_call(
        body,
        out_shape=outs[0] if single else outs,
        in_specs=[spec] * len(args),
        out_specs=spec if single else [spec] * len(outs),
        scratch_shapes=[pltpu.VMEM(t, F32) for t in scratch],
    )(*args)


def exchange(x, n):
    return lax.all_to_all(x.reshape(n, -1, HD), "chan", 0, 0).reshape(x.shape)


def swap(near, far):
    size = lax.axis_size("facet")
    apart = [(i, i + 1) for i in range(1, size - 1, 2)]
    beside = [(i, i + 1) for i in range(0, size, 2)]
    near = lax.ppermute(near, "facet", beside + [(j, i) for i, j in beside])
    far = lax.ppermute(far, "facet", apart + [(j, i) for i, j in apart])
    return near, far


def total_gram(tri, n):
    parts = tri.reshape(n, 1, -1)
    mine = jnp.sum(lax.all_to_all(parts, "chan", 0, 0), axis=0, keepdims=True)
    return lax.all_to_all(jnp.broadcast_to(mine, parts.shape), "chan", 0, 0).reshape(tri.shape)


def tables(margin, blend_table, tau_steps):
    facet_id = lax.axis_index("facet")
    facet_total = lax.axis_size("facet")
    row_index = jnp.arange(HD + 2 * OV, dtype=jnp.int32)[None, :]
    keep_all = (
        (row_index >= OV - margin[:, None]) & (row_index < HD + OV + margin[:, None])
    ).astype(F32)
    weight_all = blend_table.astype(F32) * keep_all
    row_weight = weight_all[facet_id]
    before = weight_all[:, HD:][jnp.maximum(facet_id - 1, 0)] * (facet_id > 0)
    after = weight_all[:, : 2 * OV][jnp.minimum(facet_id + 1, facet_total - 1)] * (
        facet_id < facet_total - 1
    )
    total = row_weight + jnp.pad(before, (0, HD)) + jnp.pad(after, (HD, 0))
    scale = 1.0 / jnp.where(total == 0.0, 1.0, total)
    rows = jnp.stack([keep_all[facet_id], row_weight, scale])
    center, low, high = rows[:, OV : OV + HD], rows[:, :OV], rows[:, OV + HD :]
    rows = jnp.concatenate([center, center, low, low, high, high], axis=1)
    rows = jnp.pad(rows, ((0, 5), (0, HD - 4 * OV)))
    factors = 0.1 * tau_steps.astype(F32) / math.sqrt(1.01)
    return rows + jnp.pad(factors, (3, 5 - tau_steps.shape[0]))[:, None]


def per_device(estimate, dirty, weights, margin, blend_table, tau_steps):
    n = lax.axis_size("chan")
    c, width = n * CL, (WL + 1) * HD
    assert estimate.shape == (CL, n * WL, HD)
    flat = (CL * WL * n, HD)
    small = (margin.reshape(1, -1), blend_table, tau_steps.reshape(1, -1))
    whole = pl.BlockSpec(memory_space=pltpu.VMEM)
    sent, margin, blend_table, tau_steps = pl.pallas_call(
        pack_body,
        out_shape=[pltpu.VMEM((ARRAYS * G8 * n, HD), F32)] + [pltpu.VMEM(v.shape, jnp.int32) for v in small],
        in_specs=[pl.BlockSpec(memory_space=pl.ANY)] * (ARRAYS + 3),
        out_specs=[whole] * 4,
        scratch_shapes=[pltpu.VMEM((ARRAYS,) + flat, F32), pltpu.SemaphoreType.DMA((ARRAYS, CL)), pltpu.SemaphoreType.DMA((3,))],
        name="pack",
    )(estimate.reshape(flat), dirty.reshape(flat), weights.reshape(flat), *small)
    got = exchange(sent, n)
    near, far = run(edge_body, [(2 * n, HD)] * 2, got)
    near, far = swap(near, far)
    table = tables(margin[0], blend_table, tau_steps[0])
    sums = (n * pl.cdiv(c * (c + 1) // 2, n * HD), HD)
    x, gram = run(gram_body, [(c, width), sums], got, near, far, table)
    gram = total_gram(gram, n)
    s, s_near, s_far = run(zone_body, [(c, width), (2 * n, HD), (2 * n, HD)], gram, x, got, table, scratch=[(c, c)])
    s_near, s_far = swap(s_near, s_far)
    x, gram = run(next_body, [(c, width), sums], got, near, far, s, s_near, s_far, table)
    gram = total_gram(gram, n)
    kernel, s_near, s_far = run(last_body, [(c, c), (n, HD), (n, HD)], gram, x, table, scratch=[(c, c), (c, HD)])
    s = run(center_body, [(c, WL * HD)], kernel, x, table)
    s_near, s_far = swap(s_near, s_far)
    back = exchange(run(close_body, [(G8 * n, HD)], s, s_near, s_far, table), n)
    return run(unpack_body, [flat], back, leave=False).reshape(estimate.shape)


def solution(mesh):
    placed = (
        P("chan", None, "facet"),
        P("chan", None, "facet"),
        P("chan", None, "facet"),
        P(),
        P(),
        P(),
    )

    return jax.shard_map(per_device, mesh=mesh, in_specs=placed, out_specs=P("chan", None, "facet"), check_vma=False)
```

```python
import math

import jax
import jax.numpy as jnp
from jax import lax
from jax.experimental import pallas as pl
from jax.experimental.pallas import tpu as pltpu
from jax.sharding import PartitionSpec as P


OV = 16
CL = 4
WL = 2
HD = 128
G8 = CL * WL
ARRAYS = 3
F32 = jnp.float32


def lanes(shape):
    return lax.broadcasted_iota(jnp.int32, shape, 1)


def shift(x, by):
    by %= x.shape[1]
    return pltpu.roll(x, by, 1) if by else x


def pack_center(pieces, offset):
    group = lanes(pieces[0].shape) // OV
    out = shift(pieces[0], -offset)
    for g in range(1, G8):
        out = jnp.where(group == g, shift(pieces[g], OV * g - offset), out)
    return out


def pack_edges(edges, offset):
    group = lanes(edges[0].shape) // (WL * OV)
    out = shift(edges[0], -offset)
    for c in range(1, CL):
        out = jnp.where(group == c, shift(edges[c], WL * OV * c - offset), out)
    return out


def open_edges(before, after, c):
    lane = lanes(before.shape)
    step = WL * OV
    rest = jnp.where(lane < 2 * step, shift(after, step - step * c), 0.0)
    return jnp.where(lane < step, shift(before, -step * c), rest)


def open_center(before, after, g):
    lane = lanes(before.shape)
    rest = jnp.where(lane >= HD - OV, shift(after, HD - OV - OV * g), 0.0)
    return jnp.where(lane < OV, shift(before, -OV * g), rest)


def split(x):
    top = x.astype(jnp.bfloat16)
    return top, (x - top.astype(F32)).astype(jnp.bfloat16)


def product(a, b, contract=((1,), (0,))):
    dims = (contract, ((), ()))
    parts = ((a[0], b[1]), (a[1], b[0]), (a[0], b[0]))
    p, q, r = (lax.dot_general(u, v, dims, preferred_element_type=F32) for u, v in parts)
    return p + q + r


def put_gram(x, tri):
    half = x.shape[0] // 2
    parts = split(x[...])
    low, high = ([p[i * half : i * half + half, :] for p in parts] for i in (0, 1))
    rows = ((1,), (1,))
    first, second = product(low, low, rows), product(high, high, rows)
    row = lax.broadcasted_iota(jnp.int32, first.shape, 0)
    col = lanes(first.shape)
    tri[0:half, :] = product(low, high, rows)
    tri[half : 2 * half, :] = jnp.where(row >= col, first, second)
    diagonal = jnp.sum(jnp.where(row == col, second, 0.0), axis=0, keepdims=True)
    rest = (tri.shape[0] - 2 * half, half)
    tri[2 * half :, :] = jnp.where(lax.broadcasted_iota(jnp.int32, rest, 0) == 0, diagonal, 0.0)


def get_gram(tri, gram):
    half = gram.shape[0] // 2
    above, both = tri[0:half, :], tri[half : 2 * half, :]
    row = lax.broadcasted_iota(jnp.int32, both.shape, 0)
    col = lanes(both.shape)
    turned = both.T
    gram[0:half, 0:half] = jnp.where(row >= col, both, turned)
    gram[0:half, half:] = above
    gram[half:, 0:half] = above.T
    diagonal = jnp.where(row == col, tri[2 * half : 2 * half + 1, :], turned)
    gram[half:, half:] = jnp.where(row < col, both, diagonal)
    return gram[...]


def pack_body(est, dirty, weights, margin, blend, tau, out, margin_out, blend_out, tau_out, buf, sems, small):
    n = out.shape[0] // (ARRAYS * G8)
    copies = []
    for c in range(CL):
        rows = pl.ds(c * WL * n, WL * n)
        for a, ref in enumerate((est, dirty, weights)):
            copies.append(pltpu.make_async_copy(ref.at[rows, :], buf.at[a, rows, :], sems.at[a, c]))
            copies[-1].start()
    for i, pair in enumerate(((margin, margin_out), (blend, blend_out), (tau, tau_out))):
        copies.append(pltpu.make_async_copy(*pair, small.at[i]))
        copies[-1].start()
    for c in range(CL):
        for a in range(ARRAYS):
            copies[c * ARRAYS + a].wait()
        for w in range(WL):
            rows = pl.ds(c * WL * n + w, n, stride=WL)
            e, d, k = buf[0, rows, :], buf[1, rows, :], buf[2, rows, :]
            for a, value in enumerate((e - k * (e - d), d, k)):
                out[pl.ds(a * G8 + c * WL + w, n, stride=ARRAYS * G8), :] = value
    for copy in copies[CL * ARRAYS :]:
        copy.wait()


def is_even():
    return lax.axis_index("facet") % 2 == 0


def give(low, high):
    even = is_even()
    return jnp.where(even, high, low), jnp.where(even, low, high)


def take(near, far):
    even = is_even()
    return jnp.where(even, far, near), jnp.where(even, near, far)


def piece(got, a, g):
    n = got.shape[0] // (ARRAYS * G8)
    return got[pl.ds(a * G8 + g, n, stride=ARRAYS * G8), :]


def edge_body(got, near, far):
    n = near.shape[0] // 2
    for i, a in enumerate((0, 2)):
        pieces = [piece(got, a, g) for g in range(G8)]
        rows = pl.ds(i * n, n)
        near[rows, :], far[rows, :] = give(pack_center(pieces, 0), pack_center(pieces, HD - OV))


def inner_body(got, x, tri):
    n = got.shape[0] // (ARRAYS * G8)
    for c in range(CL):
        for w in range(WL):
            x[pl.ds(c * n, n), pl.ds(w * HD, HD)] = piece(got, 0, c * WL + w)
    put_gram(x, tri)


def gram_body(inner, near, far, table, edges, tri):
    n = near.shape[0] // 2
    keep = table[0:1, WL * HD :]
    before, after = take(near[0:n, :], far[0:n, :])
    for c in range(CL):
        edges[pl.ds(c * n, n), :] = open_edges(before, after, c) * keep
    put_gram(edges, tri)
    tri[...] += inner[...]


def kernel_of(gram, factor):
    count = gram.shape[0]
    row = lax.broadcasted_iota(jnp.int32, gram.shape, 0)
    identity = (row == lanes(gram.shape)).astype(F32)
    trace = jnp.sum(jnp.sum(gram * identity, axis=1, keepdims=True), axis=0, keepdims=True)
    mean_eigen = trace / count + 1e-06
    target = (gram + (0.01 * mean_eigen) * identity) / (16.16 * mean_eigen)
    first = 1.5 * identity - 0.5 * target
    parts = split(target)
    square = product(parts, parts)
    stepped = 1.5 * target - 0.5 * square
    twice = 2.25 * identity - 1.5 * target + 0.25 * square
    inverse_root = 1.5 * first - 0.5 * product(split(stepped), split(twice))
    return identity - factor * inverse_root


def put_rims(edges, n, near, far):
    edges = [edges[pl.ds(c * n, n), :] for c in range(CL)]
    near[0:n, :], far[0:n, :] = give(pack_edges(edges, 0), pack_edges(edges, WL * OV))


def zone_body(tri, x, rims, got, table, out, near, far, gram):
    n = x.shape[0] // CL
    kernel = split(kernel_of(get_gram(tri, gram), table[3:4, : gram.shape[0]]))
    for cols, part in ((slice(0, WL * HD), x), (slice(WL * HD, WL * HD + HD), rims)):
        out[:, cols] = product(kernel, split(part[...])) * table[1:2, cols]
    put_rims(out.at[:, pl.ds(WL * HD, HD)], n, near, far)
    pieces = []
    for g in range(G8):
        cols = pl.ds(g % WL * HD, HD)
        d, k = piece(got, 1, g), piece(got, 2, g)
        own = out[pl.ds(g // WL * n, n), cols] * table[2:3, :HD]
        pieces.append(own - k * (own - d))
    rows = slice(n, 2 * n)
    near[rows, :], far[rows, :] = give(pack_center(pieces, 0), pack_center(pieces, HD - OV))


def next_body(got, near, far, s, s_near, s_far, table, x, tri):
    n = near.shape[0] // 2
    keep = table[0:1, WL * HD :]
    scale = table[2:3, :]
    center = take(s_near[0:n, :], s_far[0:n, :])
    outer = take(s_near[n : 2 * n, :], s_far[n : 2 * n, :])
    k_edges = take(near[n : 2 * n, :], far[n : 2 * n, :])
    for c in range(CL):
        rows = pl.ds(c * n, n)
        for w in range(WL):
            g = c * WL + w
            cols = slice(w * HD, w * HD + HD)
            d, k = piece(got, 1, g), piece(got, 2, g)
            current = (s[rows, cols] + open_center(*center, g)) * scale[:, cols]
            x[rows, cols] = current - k * (current - d)
        cols = slice(WL * HD, WL * HD + HD)
        own = s[rows, cols] * scale[:, cols]
        x[rows, cols] = (own - open_edges(*k_edges, c) * own + open_edges(*outer, c)) * keep
    put_gram(x, tri)


def last_body(tri, x, table, kernel, near, far, gram, edges):
    kernel[...] = kernel_of(get_gram(tri, gram), table[4:5, : gram.shape[0]])
    edges[...] = product(split(kernel[...]), split(x[:, WL * HD :])) * table[1:2, WL * HD :]
    put_rims(edges, x.shape[0] // CL, near, far)


def center_body(kernel, x, table, out):
    out[...] = product(split(kernel[...]), split(x[:, : WL * HD])) * table[1:2, : WL * HD]


def close_body(s, near, far, table, out):
    n = near.shape[0]
    center = take(near[...], far[...])
    for c in range(CL):
        for w in range(WL):
            g = c * WL + w
            total = s[pl.ds(c * n, n), pl.ds(w * HD, HD)] + open_center(*center, g)
            out[pl.ds(g, n, stride=G8), :] = total * table[2:3, w * HD : w * HD + HD]


def unpack_body(got, out):
    n = got.shape[0] // G8
    for c in range(CL):
        for w in range(WL):
            out[pl.ds(c * WL * n + w, n, stride=WL), :] = got[pl.ds(c * WL + w, n, stride=G8), :]


def run(body, shapes, *args, leave=True, scratch=()):
    spec = pl.BlockSpec(memory_space=pltpu.VMEM)
    outs = [pltpu.VMEM(s, F32) if leave else jax.ShapeDtypeStruct(s, F32) for s in shapes]
    single = len(outs) == 1
    args = [pltpu.with_memory_space_constraint(a, pltpu.VMEM) for a in args]
    return pl.pallas_call(
        body,
        out_shape=outs[0] if single else outs,
        in_specs=[spec] * len(args),
        out_specs=spec if single else [spec] * len(outs),
        scratch_shapes=[pltpu.VMEM(t, F32) for t in scratch],
    )(*args)


def exchange(x, n):
    return lax.all_to_all(x.reshape(n, -1, HD), "chan", 0, 0).reshape(x.shape)


def swap(near, far):
    size = lax.axis_size("facet")
    apart = [(i, i + 1) for i in range(1, size - 1, 2)]
    beside = [(i, i + 1) for i in range(0, size, 2)]
    near = lax.ppermute(near, "facet", beside + [(j, i) for i, j in beside])
    far = lax.ppermute(far, "facet", apart + [(j, i) for i, j in apart])
    return near, far


def total_gram(tri, n):
    parts = tri.reshape(n, 1, -1)
    mine = jnp.sum(lax.all_to_all(parts, "chan", 0, 0), axis=0, keepdims=True)
    return lax.all_to_all(jnp.broadcast_to(mine, parts.shape), "chan", 0, 0).reshape(tri.shape)


def tables(margin, blend_table, tau_steps):
    facet_id = lax.axis_index("facet")
    facet_total = lax.axis_size("facet")
    row_index = jnp.arange(HD + 2 * OV, dtype=jnp.int32)[None, :]
    keep_all = (
        (row_index >= OV - margin[:, None]) & (row_index < HD + OV + margin[:, None])
    ).astype(F32)
    weight_all = blend_table.astype(F32) * keep_all
    row_weight = weight_all[facet_id]
    before = weight_all[:, HD:][jnp.maximum(facet_id - 1, 0)] * (facet_id > 0)
    after = weight_all[:, : 2 * OV][jnp.minimum(facet_id + 1, facet_total - 1)] * (
        facet_id < facet_total - 1
    )
    total = row_weight + jnp.pad(before, (0, HD)) + jnp.pad(after, (HD, 0))
    scale = 1.0 / jnp.where(total == 0.0, 1.0, total)
    rows = jnp.stack([keep_all[facet_id], row_weight, scale])
    center, low, high = rows[:, OV : OV + HD], rows[:, :OV], rows[:, OV + HD :]
    rows = jnp.concatenate([center, center, low, low, high, high], axis=1)
    rows = jnp.pad(rows, ((0, 5), (0, HD - 4 * OV)))
    factors = 0.1 * tau_steps.astype(F32) / math.sqrt(1.01)
    return rows + jnp.pad(factors, (3, 5 - tau_steps.shape[0]))[:, None]


def per_device(estimate, dirty, weights, margin, blend_table, tau_steps):
    n = lax.axis_size("chan")
    c, width = n * CL, (WL + 1) * HD
    assert estimate.shape == (CL, n * WL, HD)
    flat = (CL * WL * n, HD)
    small = (margin.reshape(1, -1), blend_table, tau_steps.reshape(1, -1))
    whole = pl.BlockSpec(memory_space=pltpu.VMEM)
    sent, margin, blend_table, tau_steps = pl.pallas_call(
        pack_body,
        out_shape=[pltpu.VMEM((ARRAYS * G8 * n, HD), F32)] + [pltpu.VMEM(v.shape, jnp.int32) for v in small],
        in_specs=[pl.BlockSpec(memory_space=pl.ANY)] * (ARRAYS + 3),
        out_specs=[whole] * 4,
        scratch_shapes=[pltpu.VMEM((ARRAYS,) + flat, F32), pltpu.SemaphoreType.DMA((ARRAYS, CL)), pltpu.SemaphoreType.DMA((3,))],
        name="pack",
    )(estimate.reshape(flat), dirty.reshape(flat), weights.reshape(flat), *small)
    got = exchange(sent, n)
    near, far = run(edge_body, [(2 * n, HD)] * 2, got)
    near, far = swap(near, far)
    table = tables(margin[0], blend_table, tau_steps[0])
    sums = (n * pl.cdiv(c * (c + 1) // 2, n * HD), HD)
    x, inner = run(inner_body, [(c, WL * HD), sums], got)
    rims, gram = run(gram_body, [(c, HD), sums], inner, near, far, table)
    gram = total_gram(gram, n)
    s, s_near, s_far = run(
        zone_body, [(c, width), (2 * n, HD), (2 * n, HD)], gram, x, rims, got, table, scratch=[(c, c)]
    )
    s_near, s_far = swap(s_near, s_far)
    x, gram = run(next_body, [(c, width), sums], got, near, far, s, s_near, s_far, table)
    gram = total_gram(gram, n)
    kernel, s_near, s_far = run(last_body, [(c, c), (n, HD), (n, HD)], gram, x, table, scratch=[(c, c), (c, HD)])
    s = run(center_body, [(c, WL * HD)], kernel, x, table)
    s_near, s_far = swap(s_near, s_far)
    back = exchange(run(close_body, [(G8 * n, HD)], s, s_near, s_far, table), n)
    return run(unpack_body, [flat], back, leave=False).reshape(estimate.shape)


def solution(mesh):
    placed = (
        P("chan", None, "facet"),
        P("chan", None, "facet"),
        P("chan", None, "facet"),
        P(),
        P(),
        P(),
    )

    return jax.shard_map(per_device, mesh=mesh, in_specs=placed, out_specs=P("chan", None, "facet"), check_vma=False)
```
